32 devices in a mesh: row: 4 (over x, core), col: 2 (over y), store: 4 (over z).
Axes of the slice: x: 2, y: 2, z: 4, core: 2. Of those that a mesh axis runs over, the one named last changes fastest.
Arguments:
- hidden: bfloat16 [128, 128, 4096], P('store', 'row', 'col'), may hold values from -6 to 6
- out_grads: bfloat16 [208, 128, 128], P('row', 'store'), may hold values from -6 to 6
- proj_out: bfloat16 [208, 64], P('row'), may hold values from -0.4375 to 0.4375
- proj_in: bfloat16 [4096, 64], P('col'), may hold values from -0.09375 to 0.09375
- lengths: int32 [128], P('store'), may hold values from 64 to 128
- precond: bfloat16 [4096, 4096], P(('row', 'col'), 'store'), may hold values from -1 to 2, as said below
- stored: bfloat16 [12288, 4096], P(('row', 'col', 'store')), may hold values from -0.09375 to 0.09375
Outputs:
- scores: float32 [128, 12288], P(None, ('row', 'col', 'store'))
The draws below stay inside these ranges and needn't reach their ends.
Inputs may be any that keep to these rules, and one draw needn't show every extreme that they name: Query q's live tokens are its first lengths[q] token slots. precond is symmetric.
All inputs are finite; a program needn't handle non-finite values.
Results may differ from the reference program's by a relative error of at most 0.0057.
Values may be sent and summed in bfloat16 or wider, within the bound.
No kernel may reach another device: no remote copies, remote signals or barrier semaphores. Data moves between devices by JAX's collectives and lax.ppermute only.
A program may use at most 64 MiB of HBM per device.

```python
import math
import jax
import jax.numpy as jnp
from jax import lax

C = 4096
R = 208
PA = 64
PB = 64
TOK = 128
ROWS = 384
K = 4096
NQ = 128
NS = 12288
N_ROW = 4
N_COL = 2


def draw_precond(key, part):
    noise = jax.random.uniform(jax.random.fold_in(key, 17), (K, K), jnp.float32, -1.0, 1.0)
    symmetric = (noise + noise.T) / math.sqrt(K)
    matrix = symmetric + jnp.eye(K, dtype=jnp.float32)
    return matrix.astype(jnp.bfloat16)


def plant(values, rng, least, top_value):
    shape = values.shape
    index_at = [jax.random.randint(jax.random.fold_in(rng, axis), (), 0, shape[axis]) for axis in range(len(shape))]
    values = values.at[tuple(index_at)].set(least)
    longest = shape.index(max(shape))
    index_at[longest] = (index_at[longest] + 1) % shape[longest]
    return values.at[tuple(index_at)].set(top_value)


def level_of(own_key, shape, cuts, low, largest):
    def one(dim, parts):
        steps = jax.random.uniform(jax.random.fold_in(jax.random.fold_in(own_key, 6), dim), (parts,), jnp.float32, low / len(cuts), largest / len(cuts))
        return jnp.repeat(jnp.exp(steps), shape[dim] // parts).reshape((-1,) + (1,) * (len(shape) - dim - 1))

    level = one(*cuts[0])
    for cut in cuts[1:]:
        level = level * one(*cut)
    return level


def normal_values(key, extent, deviation, most, cuts=(), held_as=jnp.bfloat16):
    values = deviation * jax.random.normal(key, extent, jnp.float32)
    if cuts:
        values = values * level_of(key, extent, cuts, -0.22, 0.18)
    return jnp.clip(values, -most, most).astype(held_as)


def setup_inputs(seed: int = 0) -> dict:
    key_list = jax.random.split(jax.random.key(seed), 8)
    return {
        "hidden": normal_values(key_list[0], (NQ, TOK, C), 1.0, 6.0, ((0, 4), (1, 4), (2, 2))),
        "out_grads": normal_values(key_list[1], (R, NQ, TOK), 1.0, 6.0, ((0, 4), (1, 4))),
        "proj_out": normal_values(key_list[2], (R, PA), R ** -0.5, 0.4375, ((0, 4),)),
        "proj_in": normal_values(key_list[3], (C, PB), C ** -0.5, 0.09375, ((0, 2),)),
        "lengths": plant(jax.random.randint(key_list[4], (NQ,), TOK // 2, TOK + 1), jax.random.fold_in(key_list[4], 1), TOK // 2, TOK).astype(jnp.int32),
        "precond": draw_precond(jax.random.fold_in(key_list[7], 71), 0),
        "stored": normal_values(key_list[6], (NS, K), K ** -0.5, 0.09375, ((0, 32),)),
    }


def reference(hidden, out_grads, proj_out, proj_in, lengths, precond, stored):
    rows_block = R // N_ROW
    cols_block = C // N_COL
    position = jnp.arange(TOK, dtype=jnp.int32)
    live_mask = (position[None, :] < lengths[:, None]).astype(jnp.float32)
    u_total = jnp.zeros((NQ, TOK, PA), jnp.float32)
    for row_block in range(N_ROW):
        grads_part = out_grads[row_block * rows_block:(row_block + 1) * rows_block].astype(jnp.float32)
        weights_part = proj_out[row_block * rows_block:(row_block + 1) * rows_block].astype(jnp.float32)
        projected = jnp.einsum("rqt,ra->qta", grads_part, weights_part) * live_mask[:, :, None]
        u_total = u_total + lax.optimization_barrier(projected.astype(jnp.bfloat16)).astype(jnp.float32)
    v_total = jnp.zeros((NQ, TOK, PB), jnp.float32)
    for col_block in range(N_COL):
        inputs_part = hidden[:, :, col_block * cols_block:(col_block + 1) * cols_block].astype(jnp.float32)
        weights_part = proj_in[col_block * cols_block:(col_block + 1) * cols_block].astype(jnp.float32)
        projected = jnp.einsum("qtc,cb->qtb", inputs_part, weights_part)
        v_total = v_total + lax.optimization_barrier(projected.astype(jnp.bfloat16)).astype(jnp.float32)
    features = jnp.einsum("qta,qtb->qab", u_total, v_total).reshape(NQ, K) * (TOK ** -0.5)
    features_b = features.astype(jnp.bfloat16)
    conditioned = jnp.dot(features_b, precond, preferred_element_type=jnp.float32).astype(jnp.bfloat16)
    stacked = stored.reshape(NS // ROWS, ROWS, K)

    def score_part(stored_part):
        return lax.dot_general(conditioned, stored_part, (((1,), (1,)), ((), ())), preferred_element_type=jnp.float32)

    score_parts = lax.map(score_part, stacked)
    return jnp.transpose(score_parts, (1, 0, 2)).reshape(NQ, NS)
```

```python
import functools

import jax
import jax.numpy as jnp
from jax import lax
from jax.experimental import pallas as pl
from jax.experimental.pallas import tpu as pltpu
from jax.sharding import PartitionSpec as P

F32 = jnp.float32
BF16 = jnp.bfloat16
AXES = ("row", "col", "store")
NT = (((1,), (1,)), ((), ()))
NN = (((1,), (0,)), ((), ()))
VMEM = pl.BlockSpec(memory_space=pltpu.VMEM)
SMEM = pl.BlockSpec(memory_space=pltpu.SMEM)


def dot(a, b, dims):
    return lax.dot_general(a, b, dims, preferred_element_type=F32)


def project_kernel(n_col, lengths, hidden, proj_in_t, grads, proj_out, out, grads_f32, weights):
    dest = pl.program_id(0)
    rows, queries, tokens = grads.shape
    q_dest, t_part, columns = hidden.shape
    width = proj_out.shape[1]

    @pl.when(dest == 0)
    def _():
        grads_f32[...] = grads[...].astype(F32).reshape(rows * queries, tokens)
        i = lax.broadcasted_iota(jnp.int32, (width, width), 0)
        j = lax.broadcasted_iota(jnp.int32, (width, width), 1)
        half = width // 2
        pick = j == jnp.where(i < half, 2 * i, 2 * (i - half) + 1)
        weights[...] = dot(pick.astype(BF16), proj_out[...], NT).astype(BF16)

    v = dot(proj_in_t[...], hidden[...].reshape(q_dest * t_part, columns), NT)
    width_in = v.shape[0]
    out[0, 0:width_in, :] = v.astype(BF16)
    share = q_dest // n_col
    lane = lax.broadcasted_iota(jnp.int32, (width, tokens), 1)
    for i in range(share):
        q = dest * q_dest + lax.axis_index("col") * share + i
        g = grads_f32[pl.ds(q, rows, stride=queries), :].astype(BF16)
        u = dot(weights[...], g, NN)
        u = jnp.where(lane < lengths[q], u, 0.0)
        at = width_in + i * width
        out[0, at : at + width, :] = u.astype(BF16)


def feature_kernel(n_row, n_col, q_dest, width, width_in, copies, got, out, held):
    tokens = got.shape[2]
    t_part = tokens // q_dest
    share = q_dest // n_col
    half = width // 2
    scale = tokens ** (-0.5)
    lane_v = lax.broadcasted_iota(jnp.int32, (width_in, tokens), 1)
    parts = [[got[b * n_col + c, 0:width_in, :].astype(F32) for b in range(n_row)] for c in range(n_col)]
    lane_f = lax.broadcasted_iota(jnp.int32, (half, n_col * width_in), 1)
    for q in range(q_dest):
        v_rows = []
        for c in range(n_col):
            v = None
            for b in range(n_row):
                shift = ((b - q) * t_part) % tokens
                part = pltpu.roll(parts[c][b], shift, 1) if shift else parts[c][b]
                v = part if v is None else jnp.where(lane_v >= b * t_part, part, v)
            v_rows.append(v)
        v_all = jnp.concatenate(v_rows, axis=0).astype(BF16)
        at = width_in + (q % share) * width
        total = None
        for b in range(n_row):
            u = got[b * n_col + q // share, at : at + width, :]
            term = dot(u, v_all, NT)
            total = term if total is None else total + term
        total = total + pltpu.roll(total, width_in, 1)
        packed = jnp.where(lane_f < width_in, total[:half], total[half:]) * scale
        held[pl.ds(q, half, stride=q_dest), :] = packed
    n = held.shape[0] // n_row
    for r in range(n_row):
        block = held[r * n : (r + 1) * n, :].astype(BF16)
        for k in range(copies):
            out[r * copies + k] = block


def condition_kernel(n_row, n_col, q_dest, got, p_own, p_got, keep, send, got_f32):
    sources, rows, lanes = got.shape
    got_f32[...] = got[...].astype(F32).reshape(sources * rows, lanes)
    col = lax.axis_index("col")
    core = lax.rem(lax.axis_index("row"), 2)
    pairs = rows // q_dest
    here = pairs // n_col
    depth, width = p_got.shape
    mine = pl.ds(pl.multiple_of(col * width, width), width)

    def features(side, half):
        columns = []
        for i in range(here):
            blocks = []
            for h in range(q_dest // 2):
                at = (half * here + i) * q_dest + 2 * h + side
                blocks.append(got_f32[pl.ds(at, sources, stride=rows), :])
            columns.append(jnp.concatenate(blocks, axis=0).astype(BF16))
        return jnp.concatenate(columns, axis=1)

    for ref, side in ((send, 1 - core), (keep, core)):
        acc = dot(features(side, col), p_own[:, mine], NN)
        acc += dot(features(side, 1 - col), p_got[...], NN)
        ref[...] = acc.reshape(ref.shape)


def fold_kernel(keep, got, mine, other):
    x = lax.axis_index("row") // 2
    other[...] = keep[1 - x] + got[1 - x]
    mine[...] = keep[x] + got[x]


def finish_kernel(mine, got, out):
    out[...] = (mine[...] + got[...]).astype(BF16)


def score_kernel(n_row, n_col, n_store, q_dest, near, far, stored, out, held, ordered):
    sources, width = near.shape[2:]
    row, col, store = (lax.axis_index(a) for a in AXES)
    x, core = row // 2, lax.rem(row, 2)
    n_x = n_row // 2
    acc = None
    for iy in range(n_col):
        for iz in range(n_store):
            y, z = lax.bitwise_xor(col, iy), lax.bitwise_xor(store, iz)
            at = pl.multiple_of((z * n_col + y) * width, width)
            left = jnp.concatenate([ref[ix * n_col + iy, iz] for ref in (near, far) for ix in range(n_x)], axis=0)
            term = dot(left, stored[:, pl.ds(at, width)], NT)
            acc = term if acc is None else acc + term
    lanes = held.shape[2]
    for i in range(held.shape[0]):
        held[i] = acc[:, i * lanes : (i + 1) * lanes]
    group = n_row * n_col
    for i in range(held.shape[0]):
        for side in range(2):
            for ix in range(n_x):
                q4 = lax.bitwise_xor(x, ix) * 2 + lax.bitwise_xor(core, side)
                base = (side * n_x + ix) * sources
                for s in range(n_store):
                    rows = held[i, pl.ds(base + s, group, stride=n_store), :]
                    ordered[i, pl.ds(s * group * q_dest + q4, group, stride=q_dest), :] = rows
        out[:, i * lanes : (i + 1) * lanes] = ordered[i]


def call(kernel, outs, in_specs, scratch=(), flops=0, size=0, **more):
    return pl.pallas_call(
        kernel,
        out_shape=outs,
        in_specs=in_specs,
        scratch_shapes=list(scratch),
        cost_estimate=pl.CostEstimate(flops=flops, bytes_accessed=size, transcendentals=0),
        **more,
    )


def shape(s, t):
    return jax.ShapeDtypeStruct(s, t)


def swap(x, axis, n, k):
    return lax.ppermute(x, axis, [(i, i ^ k) for i in range(n)])


def split_device(sizes, hidden, out_grads, proj_out, proj_in, lengths, precond, stored):
    n_row, n_col, n_store = sizes
    group = n_row * n_col
    queries, t_part, columns = hidden.shape
    rows, _, tokens = out_grads.shape
    width, width_in = proj_out.shape[1], proj_in.shape[1]
    q_dest = queries // group
    share = q_dest // n_col
    depth = width_in + share * width
    col = lax.axis_index("col")
    j_width = precond.shape[1] // n_col

    p_send = lax.dynamic_slice_in_dim(precond, (1 - col) * j_width, j_width, axis=1)
    p_got = swap(p_send, "col", n_col, 1)

    const = lambda nd: (lambda i: (0,) * nd)
    blocks = pl.pallas_call(
        functools.partial(project_kernel, n_col),
        grid=(group,),
        in_specs=[
            SMEM,
            pl.BlockSpec((q_dest, t_part, columns), lambda i: (i, 0, 0)),
            pl.BlockSpec((width_in, columns), const(2)),
            pl.BlockSpec(out_grads.shape, const(3)),
            pl.BlockSpec(proj_out.shape, const(2)),
        ],
        out_specs=pl.BlockSpec((1, depth, tokens), lambda i: (i, 0, 0)),
        out_shape=shape((group, depth, tokens), BF16),
        scratch_shapes=[pltpu.VMEM((rows * queries, tokens), F32), pltpu.VMEM((width, rows), BF16)],
        cost_estimate=pl.CostEstimate(flops=2 * hidden.size * width_in, bytes_accessed=2 * hidden.size, transcendentals=0),
    )(lengths, hidden, proj_in.T, out_grads, proj_out)
    got = lax.all_to_all(blocks, ("row", "col"), 0, 0)

    copies = n_col * n_store
    half = width // 2
    n = half * q_dest // n_row
    feats = call(
        functools.partial(feature_kernel, n_row, n_col, q_dest, width, width_in, copies),
        shape((n_row * copies, n, tokens), BF16),
        [VMEM],
        [pltpu.VMEM((half * q_dest, tokens), F32)],
        size=2 * got.size,
    )(got)
    feats = lax.all_to_all(feats, AXES, 0, 0)

    sources = group * n_store
    part = shape((q_dest // 2, sources, j_width), F32)
    keep, send = call(
        functools.partial(condition_kernel, n_row, n_col, q_dest),
        (part, part),
        [VMEM, VMEM, VMEM],
        [pltpu.VMEM((sources * n, tokens), F32)],
        size=2 * precond.size,
    )(feats, precond, p_got)
    got = swap(send, "row", n_row, 1)
    piece = shape((sources, j_width), F32)
    mine, other = call(fold_kernel, (piece, piece), [VMEM, VMEM], size=keep.size * 8)(keep, got)
    got = swap(other, "row", n_row, 2)
    cond = call(finish_kernel, shape(piece.shape, BF16), [VMEM, VMEM], size=mine.size * 8)(mine, got)

    cond = jnp.stack([cond] + [swap(cond, "store", n_store, k) for k in range(1, n_store)])
    pairs = lambda a, k: [(i, i ^ k) for i in range(a)]
    diag = [(r * n_col + c, (r ^ 2) * n_col + (c ^ 1)) for r in range(n_row) for c in range(n_col)]
    near = jnp.stack(
        [
            cond,
            swap(cond, "col", n_col, 1),
            swap(cond, "row", n_row, 2),
            lax.ppermute(cond, ("row", "col"), diag),
        ]
    )
    far = swap(near, "row", n_row, 1)
    return call(
        functools.partial(score_kernel, n_row, n_col, n_store, q_dest),
        shape((sources * q_dest, stored.shape[0]), F32),
        [VMEM, VMEM, VMEM],
        [pltpu.VMEM((stored.shape[0] // 128, sources * q_dest, 128), F32)] * 2,
        size=2 * stored.size,
    )(near, far, stored)


def plain_device(hidden, out_grads, proj_out, proj_in, lengths, precond, stored):
    queries, token_part, columns = hidden.shape
    width_in = proj_in.shape[1]
    local_proj = jnp.einsum("qtc,cb->qtb", hidden, proj_in, preferred_element_type=F32).astype(BF16)
    flattened = local_proj.reshape(queries, token_part * width_in)
    inputs_all = lax.all_gather(flattened, "row", axis=1, tiled=True).reshape(queries, -1, width_in)
    tokens = inputs_all.shape[1]
    position = jnp.arange(tokens, dtype=jnp.int32)
    live_mask = (position[None, :] < lengths[:, None]).astype(F32)
    outputs_proj = jnp.einsum("rqt,ra->qta", out_grads, proj_out, preferred_element_type=F32)
    outputs_proj = (outputs_proj * live_mask[:, :, None]).astype(BF16)
    partial_value = jnp.einsum("qta,qtb->qab", outputs_proj, inputs_all, preferred_element_type=F32)
    partial_value = partial_value.reshape(queries, -1) * tokens ** (-0.5)
    shares = lax.psum_scatter(partial_value, ("row", "col"), scatter_dimension=1, tiled=True).astype(BF16)
    cond_terms = jnp.dot(shares, lax.all_gather(precond, "store", axis=1, tiled=True), preferred_element_type=F32)
    conditioned = lax.psum_scatter(cond_terms, ("row", "col"), scatter_dimension=1, tiled=True).astype(BF16)
    full_features = lax.all_gather(conditioned, ("row", "col"), axis=1, tiled=True)
    return lax.dot_general(
        lax.all_gather(full_features, "store", axis=0, tiled=True),
        stored,
        NT,
        preferred_element_type=F32,
    )


def solution(mesh):
    sizes = tuple(mesh.shape[a] for a in AXES)
    group = sizes[0] * sizes[1]

    def on_device(hidden, out_grads, proj_out, proj_in, lengths, precond, stored):
        args = (hidden, out_grads, proj_out, proj_in, lengths, precond, stored)
        queries = hidden.shape[0]
        fits = sizes[0] == 4 and sizes[1] == 2 and sizes[2] & (sizes[2] - 1) == 0
        fits = fits and queries % group == 0 and queries // group == sizes[0]
        fits = fits and proj_in.shape[1] * sizes[1] == 128 and proj_out.shape[1] * 2 == 128
        fits = fits and stored.shape[0] % 128 == 0 and out_grads.shape[2] == 128 and queries // group * hidden.shape[1] == 128
        if fits:
            return split_device(sizes, *args)
        return plain_device(*args)

    return jax.shard_map(
        on_device,
        mesh=mesh,
        in_specs=(
            P("store", "row", "col"),
            P("row", "store", None),
            P("row", None),
            P("col", None),
            P("store"),
            P(("row", "col"), "store"),
            P(("row", "col", "store"), None),
        ),
        out_specs=P(None, ("row", "col", "store")),
        check_vma=False,
    )
```

```python
import functools

import jax
import jax.numpy as jnp
from jax import lax
from jax.experimental import pallas as pl
from jax.experimental.pallas import tpu as pltpu
from jax.sharding import PartitionSpec as P

F32 = jnp.float32
BF16 = jnp.bfloat16
AXES = ("row", "col", "store")
NT = (((1,), (1,)), ((), ()))
NN = (((1,), (0,)), ((), ()))
VMEM = pl.BlockSpec(memory_space=pltpu.VMEM)
HBM = pl.BlockSpec(memory_space=pltpu.HBM)


def dot(a, b, dims):
    return lax.dot_general(a, b, dims, preferred_element_type=F32)


def project_kernel(n_row, n_col, lengths, hidden, proj_in_t, grads, proj_out, out, *scratch):
    lengths_s, hidden_s, proj_s, grads_s, weights_s, grads_f32, weights, blocks, sems, chunk_sems, out_sems = scratch
    rows, queries, tokens = grads.shape
    columns = hidden.shape[2]
    t_part = hidden.shape[1]
    width = proj_out.shape[1]
    width_in = proj_in_t.shape[0]
    group = n_row * n_col
    q_dest = queries // group
    share = q_dest // n_col
    dests = 2
    pairs = ((proj_in_t, proj_s), (proj_out, weights_s), (grads, grads_s), (lengths, lengths_s))
    small = [pltpu.make_async_copy(src, dst, sems.at[i]) for i, (src, dst) in enumerate(pairs)]
    chunks = []
    for i in range(group // dests):
        part = pl.ds(i * dests * q_dest, dests * q_dest)
        chunks.append(pltpu.make_async_copy(hidden.at[part], hidden_s.at[part], chunk_sems.at[i]))
    for copy in small + chunks:
        copy.start()
    small[0].wait()
    proj = proj_s[...].astype(F32).T.astype(BF16)
    for copy in small[1:]:
        copy.wait()
    i = lax.broadcasted_iota(jnp.int32, (width, width), 0)
    j = lax.broadcasted_iota(jnp.int32, (width, width), 1)
    half = width // 2
    pick = j == jnp.where(i < half, 2 * i, 2 * (i - half) + 1)
    weights[...] = dot(pick.astype(BF16), weights_s[...], NT).astype(BF16)
    grads_f32[...] = grads_s[...].astype(F32).reshape(rows * queries, tokens)
    lane = lax.broadcasted_iota(jnp.int32, (width, tokens), 1)
    outs = [pltpu.make_async_copy(blocks.at[g], out.at[g], out_sems.at[g]) for g in range(group)]
    for dest in range(group):
        for i in range(share):
            q = dest * q_dest + lax.axis_index("col") * share + i
            g = grads_f32[pl.ds(q, rows, stride=queries), :].astype(BF16)
            u = jnp.where(lane < lengths_s[q], dot(weights[...], g, NN), 0.0)
            at = width_in + i * width
            blocks[dest, at : at + width, :] = u.astype(BF16)
        if dest % dests == dests - 1:
            i = dest // dests
            chunks[i].wait()
            part = hidden_s[i * dests * q_dest : (i + 1) * dests * q_dest]
            v = dot(part.reshape(dests * q_dest * t_part, columns), proj, NN)
            for k in range(dests):
                g = i * dests + k
                blocks[g, 0:width_in, :] = v[k * tokens : (k + 1) * tokens].T.astype(BF16)
                outs[g].start()
    for copy in outs:
        copy.wait()


def feature_kernel(n_row, n_col, q_dest, width, width_in, copies, got, out, held, made, sem):
    tokens = got.shape[2]
    t_part = tokens // q_dest
    share = q_dest // n_col
    half = width // 2
    scale = tokens ** (-0.5)
    lane_v = lax.broadcasted_iota(jnp.int32, (width_in, tokens), 1)
    parts = [[got[b * n_col + c, 0:width_in, :].astype(F32) for b in range(n_row)] for c in range(n_col)]
    lane_f = lax.broadcasted_iota(jnp.int32, (half, n_col * width_in), 1)
    for q in range(q_dest):
        v_rows = []
        for c in range(n_col):
            v = None
            for b in range(n_row):
                shift = ((b - q) * t_part) % tokens
                part = pltpu.roll(parts[c][b], shift, 1) if shift else parts[c][b]
                v = part if v is None else jnp.where(lane_v >= b * t_part, part, v)
            v_rows.append(v)
        v_all = jnp.concatenate(v_rows, axis=0).astype(BF16)
        at = width_in + (q % share) * width
        total = None
        for b in range(n_row):
            u = got[b * n_col + q // share, at : at + width, :]
            term = dot(u, v_all, NT)
            total = term if total is None else total + term
        total = total + pltpu.roll(total, width_in, 1)
        packed = jnp.where(lane_f < width_in, total[:half], total[half:]) * scale
        held[pl.ds(q, half, stride=q_dest), :] = packed
    n = held.shape[0] // n_row
    for r in range(n_row):
        block = held[r * n : (r + 1) * n, :].astype(BF16)
        for k in range(copies):
            made[r * copies + k] = block
    copy = pltpu.make_async_copy(made, out, sem)
    copy.start()
    copy.wait()


def condition_kernel(n_row, n_col, q_dest, got, p_own, p_got, keep, send, got_f32):
    sources, rows, lanes = got.shape
    got_f32[...] = got[...].astype(F32).reshape(sources * rows, lanes)
    col = lax.axis_index("col")
    core = lax.rem(lax.axis_index("row"), 2)
    pairs = rows // q_dest
    here = pairs // n_col
    depth, width = p_got.shape
    mine = pl.ds(pl.multiple_of(col * width, width), width)

    def features(side, half):
        columns = []
        for i in range(here):
            blocks = []
            for h in range(q_dest // 2):
                at = (half * here + i) * q_dest + 2 * h + side
                blocks.append(got_f32[pl.ds(at, sources, stride=rows), :])
            columns.append(jnp.concatenate(blocks, axis=0).astype(BF16))
        return jnp.concatenate(columns, axis=1)

    for ref, side in ((send, 1 - core), (keep, core)):
        acc = dot(features(side, col), p_own[:, mine], NN)
        acc += dot(features(side, 1 - col), p_got[...], NN)
        ref[...] = acc.reshape(ref.shape)


def fold_kernel(keep, got, mine, other):
    x = lax.axis_index("row") // 2
    other[...] = keep[1 - x] + got[1 - x]
    mine[...] = keep[x] + got[x]


def finish_kernel(mine, got, out):
    out[...] = (mine[...] + got[...]).astype(BF16)


def score_kernel(n_row, n_col, n_store, q_dest, iy, last, near, far, stored, *refs):
    n_x, _, sources, width = near.shape
    row, col, store = (lax.axis_index(a) for a in AXES)
    x, core = row // 2, lax.rem(row, 2)
    acc = None
    for iz in range(n_store):
        y, z = lax.bitwise_xor(col, iy), lax.bitwise_xor(store, iz)
        at = pl.multiple_of((z * n_col + y) * width, width)
        left = jnp.concatenate([ref[ix, iz] for ref in (near, far) for ix in range(n_x)], axis=0)
        term = dot(left, stored[:, pl.ds(at, width)], NT)
        acc = term if acc is None else acc + term
    if not last:
        refs[0][...] = acc
        return
    before, out, held, ordered = refs
    acc += before[...]
    lanes = held.shape[2]
    group = n_row * n_col
    for i in range(held.shape[0]):
        held[i] = acc[:, i * lanes : (i + 1) * lanes]
    for i in range(held.shape[0]):
        for side in range(2):
            for ix in range(n_x):
                q4 = lax.bitwise_xor(x, ix) * 2 + lax.bitwise_xor(core, side)
                base = (side * n_x + ix) * sources
                for s in range(n_store):
                    rows = held[i, pl.ds(base + s, group, stride=n_store), :]
                    ordered[i, pl.ds(s * group * q_dest + q4, group, stride=q_dest), :] = rows
        out[:, i * lanes : (i + 1) * lanes] = ordered[i]


def call(kernel, outs, in_specs, scratch=(), flops=0, size=0, vmem=12, **more):
    return pl.pallas_call(
        kernel,
        out_shape=outs,
        in_specs=in_specs,
        scratch_shapes=list(scratch),
        cost_estimate=pl.CostEstimate(flops=flops, bytes_accessed=size, transcendentals=0),
        compiler_params=pltpu.CompilerParams(vmem_limit_bytes=vmem << 20),
        **more,
    )


def shape(s, t):
    return jax.ShapeDtypeStruct(s, t)


def swap(x, axis, n, k):
    return lax.ppermute(x, axis, [(i, i ^ k) for i in range(n)])


def split_device(sizes, hidden, out_grads, proj_out, proj_in, lengths, precond, stored):
    n_row, n_col, n_store = sizes
    group = n_row * n_col
    queries, t_part, columns = hidden.shape
    rows, _, tokens = out_grads.shape
    width, width_in = proj_out.shape[1], proj_in.shape[1]
    q_dest = queries // group
    share = q_dest // n_col
    depth = width_in + share * width
    col = lax.axis_index("col")
    j_width = precond.shape[1] // n_col

    p_send = lax.dynamic_slice_in_dim(precond, (1 - col) * j_width, j_width, axis=1)
    p_got = swap(p_send, "col", n_col, 1)

    blocks = call(
        functools.partial(project_kernel, n_row, n_col),
        shape((group, depth, tokens), BF16),
        [HBM] * 5,
        [
            pltpu.SMEM(lengths.shape, jnp.int32),
            pltpu.VMEM(hidden.shape, BF16),
            pltpu.VMEM((width_in, columns), BF16),
            pltpu.VMEM(out_grads.shape, BF16),
            pltpu.VMEM(proj_out.shape, BF16),
            pltpu.VMEM((rows * queries, tokens), F32),
            pltpu.VMEM((width, rows), BF16),
            pltpu.VMEM((group, depth, tokens), BF16),
            pltpu.SemaphoreType.DMA((4,)),
            pltpu.SemaphoreType.DMA((group // 2,)),
            pltpu.SemaphoreType.DMA((group,)),
        ],
        flops=2 * hidden.size * width_in,
        size=2 * hidden.size,
        out_specs=HBM,
        vmem=60,
    )(lengths, hidden, proj_in.T, out_grads, proj_out)
    got = lax.all_to_all(blocks, ("row", "col"), 0, 0)

    copies = n_col * n_store
    half = width // 2
    n = half * q_dest // n_row
    feats = call(
        functools.partial(feature_kernel, n_row, n_col, q_dest, width, width_in, copies),
        shape((n_row * copies, n, tokens), BF16),
        [VMEM],
        [pltpu.VMEM((half * q_dest, tokens), F32), pltpu.VMEM((n_row * copies, n, tokens), BF16), pltpu.SemaphoreType.DMA],
        size=2 * got.size,
        out_specs=HBM,
    )(got)
    feats = lax.all_to_all(feats, AXES, 0, 0)

    sources = group * n_store
    part = shape((q_dest // 2, sources, j_width), F32)
    keep, send = call(
        functools.partial(condition_kernel, n_row, n_col, q_dest),
        (part, part),
        [VMEM, VMEM, VMEM],
        [pltpu.VMEM((sources * n, tokens), F32)],
        size=2 * precond.size,
    )(feats, precond, p_got)
    got = swap(send, "row", n_row, 1)
    piece = shape((sources, j_width), F32)
    mine, other = call(fold_kernel, (piece, piece), [VMEM, VMEM], size=keep.size * 8)(keep, got)
    got = swap(other, "row", n_row, 2)
    cond = call(finish_kernel, shape(piece.shape, BF16), [VMEM, VMEM], size=mine.size * 8)(mine, got)

    cond = jnp.stack([cond] + [swap(cond, "store", n_store, k) for k in range(1, n_store)])
    pairs = lambda a, k: [(i, i ^ k) for i in range(a)]
    diag = [(r * n_col + c, (r ^ 2) * n_col + (c ^ 1)) for r in range(n_row) for c in range(n_col)]
    from_x = swap(cond, "row", n_row, 2)
    from_y = swap(cond, "col", n_col, 1)
    from_xy = lax.ppermute(cond, ("row", "col"), diag)
    scores = shape((sources * q_dest, stored.shape[0]), F32)
    score = functools.partial(score_kernel, n_row, n_col, n_store, q_dest)
    near = jnp.stack([cond, from_x])
    far = swap(near, "row", n_row, 1)
    part = call(functools.partial(score, 0, False), scores, [VMEM] * 3, size=stored.size)(near, far, stored)
    near = jnp.stack([from_y, from_xy])
    far = swap(near, "row", n_row, 1)
    held = pltpu.VMEM((stored.shape[0] // 128, sources * q_dest, 128), F32)
    return call(functools.partial(score, 1, True), scores, [VMEM] * 4, [held, held], size=stored.size)(near, far, stored, part)


def plain_device(hidden, out_grads, proj_out, proj_in, lengths, precond, stored):
    queries, token_part, columns = hidden.shape
    width_in = proj_in.shape[1]
    local_proj = jnp.einsum("qtc,cb->qtb", hidden, proj_in, preferred_element_type=F32).astype(BF16)
    flattened = local_proj.reshape(queries, token_part * width_in)
    inputs_all = lax.all_gather(flattened, "row", axis=1, tiled=True).reshape(queries, -1, width_in)
    tokens = inputs_all.shape[1]
    position = jnp.arange(tokens, dtype=jnp.int32)
    live_mask = (position[None, :] < lengths[:, None]).astype(F32)
    outputs_proj = jnp.einsum("rqt,ra->qta", out_grads, proj_out, preferred_element_type=F32)
    outputs_proj = (outputs_proj * live_mask[:, :, None]).astype(BF16)
    partial_value = jnp.einsum("qta,qtb->qab", outputs_proj, inputs_all, preferred_element_type=F32)
    partial_value = partial_value.reshape(queries, -1) * tokens ** (-0.5)
    shares = lax.psum_scatter(partial_value, ("row", "col"), scatter_dimension=1, tiled=True).astype(BF16)
    cond_terms = jnp.dot(shares, lax.all_gather(precond, "store", axis=1, tiled=True), preferred_element_type=F32)
    conditioned = lax.psum_scatter(cond_terms, ("row", "col"), scatter_dimension=1, tiled=True).astype(BF16)
    full_features = lax.all_gather(conditioned, ("row", "col"), axis=1, tiled=True)
    return lax.dot_general(
        lax.all_gather(full_features, "store", axis=0, tiled=True),
        stored,
        NT,
        preferred_element_type=F32,
    )


def solution(mesh):
    sizes = tuple(mesh.shape[a] for a in AXES)
    group = sizes[0] * sizes[1]

    def on_device(hidden, out_grads, proj_out, proj_in, lengths, precond, stored):
        args = (hidden, out_grads, proj_out, proj_in, lengths, precond, stored)
        queries = hidden.shape[0]
        fits = sizes[0] == 4 and sizes[1] == 2 and sizes[2] & (sizes[2] - 1) == 0
        fits = fits and queries % group == 0 and queries // group == sizes[0]
        fits = fits and proj_in.shape[1] * sizes[1] == 128 and proj_out.shape[1] * 2 == 128
        fits = fits and stored.shape[0] % 128 == 0 and out_grads.shape[2] == 128 and queries // group * hidden.shape[1] == 128
        if fits:
            return split_device(sizes, *args)
        return plain_device(*args)

    return jax.shard_map(
        on_device,
        mesh=mesh,
        in_specs=(
            P("store", "row", "col"),
            P("row", "store", None),
            P("row", None),
            P("col", None),
            P("store"),
            P(("row", "col"), "store"),
            P(("row", "col", "store"), None),
        ),
        out_specs=P(None, ("row", "col", "store")),
        check_vma=False,
    )
```

```python
import functools

import jax
import jax.numpy as jnp
from jax import lax
from jax.experimental import pallas as pl
from jax.experimental.pallas import tpu as pltpu
from jax.sharding import PartitionSpec as P

F32 = jnp.float32
BF16 = jnp.bfloat16
AXES = ("row", "col", "store")
NT = (((1,), (1,)), ((), ()))
NN = (((1,), (0,)), ((), ()))
VMEM = pl.BlockSpec(memory_space=pltpu.VMEM)
HBM = pl.BlockSpec(memory_space=pltpu.HBM)


def dot(a, b, dims):
    return lax.dot_general(a, b, dims, preferred_element_type=F32)


def project_kernel(n_row, n_col, lengths, hidden, proj_in_t, grads, proj_out, out, *scratch):
    lengths_s, hidden_s, proj_s, grads_s, weights_s, grads_f32, weights, blocks, sems, chunk_sems, out_sems = scratch
    rows, queries, tokens = grads.shape
    columns = hidden.shape[2]
    t_part = hidden.shape[1]
    width = proj_out.shape[1]
    width_in = proj_in_t.shape[0]
    group = n_row * n_col
    q_dest = queries // group
    share = q_dest // n_col
    dests = 2
    pairs = ((proj_in_t, proj_s), (proj_out, weights_s), (grads, grads_s), (lengths, lengths_s))
    small = [pltpu.make_async_copy(src, dst, sems.at[i]) for i, (src, dst) in enumerate(pairs)]
    chunks = []
    for i in range(group // dests):
        part = pl.ds(i * dests * q_dest, dests * q_dest)
        chunks.append(pltpu.make_async_copy(hidden.at[part], hidden_s.at[part], chunk_sems.at[i]))
    col = lax.axis_index("col")
    for copy in small + chunks:
        copy.start()
    small[0].wait()
    proj = proj_s[...].astype(F32).T.astype(BF16)
    for copy in small[1:]:
        copy.wait()
    i = lax.broadcasted_iota(jnp.int32, (width, width), 0)
    j = lax.broadcasted_iota(jnp.int32, (width, width), 1)
    half = width // 2
    pick = j == jnp.where(i < half, 2 * i, 2 * (i - half) + 1)
    weights[...] = dot(pick.astype(BF16), weights_s[...], NT).astype(BF16)
    grads_f32[...] = grads_s[...].astype(F32).reshape(rows * queries, tokens)
    lane = lax.broadcasted_iota(jnp.int32, (width, tokens), 1)
    outs = [pltpu.make_async_copy(blocks.at[g], out.at[g], out_sems.at[g]) for g in range(group)]
    for dest in range(group):
        for i in range(share):
            q = dest * q_dest + col * share + i
            g = grads_f32[pl.ds(q, rows, stride=queries), :].astype(BF16)
            u = jnp.where(lane < lengths_s[q], dot(weights[...], g, NN), 0.0)
            at = width_in + i * width
            blocks[dest, at : at + width, :] = u.astype(BF16)
        if dest % dests == dests - 1:
            i = dest // dests
            chunks[i].wait()
            part = hidden_s[i * dests * q_dest : (i + 1) * dests * q_dest]
            v = dot(part.reshape(dests * q_dest * t_part, columns), proj, NN)
            for k in range(dests):
                g = i * dests + k
                blocks[g, 0:width_in, :] = v[k * tokens : (k + 1) * tokens].T.astype(BF16)
                outs[g].start()
    for copy in outs:
        copy.wait()


def feature_kernel(n_row, n_col, q_dest, width, width_in, copies, got, precond, out, near, held, made, sem):
    fetch = pltpu.make_async_copy(precond, near, sem.at[1])
    fetch.start()
    tokens = got.shape[2]
    t_part = tokens // q_dest
    share = q_dest // n_col
    half = width // 2
    scale = tokens ** (-0.5)
    lane_v = lax.broadcasted_iota(jnp.int32, (width_in, tokens), 1)
    parts = [[got[b * n_col + c, 0:width_in, :].astype(F32) for b in range(n_row)] for c in range(n_col)]
    lane_f = lax.broadcasted_iota(jnp.int32, (half, n_col * width_in), 1)
    for q in range(q_dest):
        v_rows = []
        for c in range(n_col):
            v = None
            for b in range(n_row):
                shift = ((b - q) * t_part) % tokens
                part = pltpu.roll(parts[c][b], shift, 1) if shift else parts[c][b]
                v = part if v is None else jnp.where(lane_v >= b * t_part, part, v)
            v_rows.append(v)
        v_all = jnp.concatenate(v_rows, axis=0).astype(BF16)
        at = width_in + (q % share) * width
        total = None
        for b in range(n_row):
            u = got[b * n_col + q // share, at : at + width, :]
            term = dot(u, v_all, NT)
            total = term if total is None else total + term
        total = total + pltpu.roll(total, width_in, 1)
        packed = jnp.where(lane_f < width_in, total[:half], total[half:]) * scale
        held[pl.ds(q, half, stride=q_dest), :] = packed
    group = n_row * n_col
    n = held.shape[0] // group
    for r in range(group):
        block = held[r * n : (r + 1) * n, :].astype(BF16)
        for k in range(copies):
            made[r * copies + k] = block
    copy = pltpu.make_async_copy(made, out, sem.at[0])
    copy.start()
    copy.wait()
    fetch.wait()


def condition_kernel(n_row, n_col, n_store, q_dest, got, precond, keep, send, got_f32):
    sources, rows, lanes = got.shape
    got_f32[...] = got[...].astype(F32).reshape(sources * rows, lanes)
    core = lax.rem(lax.axis_index("row"), 2)
    group = n_row * n_col
    width = keep.shape[3]
    for ref, side in ((send, 1 - core), (keep, core)):
        columns = []
        for i in range(rows // q_dest):
            blocks = []
            for h in range(n_row // 2):
                for s in range(n_store):
                    at = s * rows + i * q_dest + 2 * h + side
                    blocks.append(got_f32[pl.ds(at, group, stride=n_store * rows), :])
            columns.append(jnp.concatenate(blocks, axis=0).astype(BF16))
        acc = dot(jnp.concatenate(columns, axis=1), precond[...], NN)
        for h in range(n_row // 2):
            for y in range(n_col):
                ref[h, y] = acc[h * sources : (h + 1) * sources, y * width : (y + 1) * width]


def fold_kernel(keep, got, *refs):
    x, y = lax.axis_index("row") // 2, lax.axis_index("col")
    for ref, (a, b) in zip(refs, ((x, y), (1 - x, y), (x, 1 - y), (1 - x, 1 - y))):
        ref[...] = keep[a, b] + got[a, b]


def finish_kernel(*refs):
    total = refs[0][...]
    for ref in refs[1:-1]:
        total += ref[...]
    refs[-1][...] = total.astype(BF16)


def score_kernel(n_row, n_col, n_store, q_dest, iy, last, near, far, stored, *refs):
    n_x, _, sources, width = near.shape
    row, col, store = (lax.axis_index(a) for a in AXES)
    x, core = row // 2, lax.rem(row, 2)
    acc = None
    for iz in range(n_store):
        y, z = lax.bitwise_xor(col, iy), lax.bitwise_xor(store, iz)
        at = pl.multiple_of((z * n_col + y) * width, width)
        left = jnp.concatenate([ref[ix, iz] for ref in (near, far) for ix in range(n_x)], axis=0)
        term = dot(left, stored[:, pl.ds(at, width)], NT)
        acc = term if acc is None else acc + term
    if not last:
        refs[0][...] = acc
        return
    before, out, ordered = refs
    acc += before[...]
    lanes = ordered.shape[2]
    for i in range(ordered.shape[0]):
        for side in range(2):
            for ix in range(n_x):
                q4 = lax.bitwise_xor(x, ix) * 2 + lax.bitwise_xor(core, side)
                base = (side * n_x + ix) * sources
                block = acc[base : base + sources, i * lanes : (i + 1) * lanes]
                ordered[i, pl.ds(q4, sources, stride=q_dest), :] = block
        out[:, i * lanes : (i + 1) * lanes] = ordered[i]


def call(kernel, outs, in_specs, scratch=(), flops=0, size=0, vmem=12, **more):
    return pl.pallas_call(
        kernel,
        out_shape=outs,
        in_specs=in_specs,
        scratch_shapes=list(scratch),
        cost_estimate=pl.CostEstimate(flops=flops, bytes_accessed=size, transcendentals=0),
        compiler_params=pltpu.CompilerParams(vmem_limit_bytes=vmem << 20),
        **more,
    )


def shape(s, t):
    return jax.ShapeDtypeStruct(s, t)


def swap(x, axis, n, k):
    return lax.ppermute(x, axis, [(i, i ^ k) for i in range(n)])


def split_device(sizes, hidden, out_grads, proj_out, proj_in, lengths, precond, stored):
    n_row, n_col, n_store = sizes
    group = n_row * n_col
    queries, t_part, columns = hidden.shape
    rows, _, tokens = out_grads.shape
    width, width_in = proj_out.shape[1], proj_in.shape[1]
    q_dest = queries // group
    share = q_dest // n_col
    depth = width_in + share * width
    col = lax.axis_index("col")
    j_width = precond.shape[1] // n_col

    inputs = (lengths, hidden, proj_in.T, out_grads, proj_out)
    blocks = call(
        functools.partial(project_kernel, n_row, n_col),
        pltpu.HBM((group, depth, tokens), BF16),
        [HBM] * 5,
        [
            pltpu.SMEM(lengths.shape, jnp.int32),
            pltpu.VMEM(hidden.shape, BF16),
            pltpu.VMEM((width_in, columns), BF16),
            pltpu.VMEM(out_grads.shape, BF16),
            pltpu.VMEM(proj_out.shape, BF16),
            pltpu.VMEM((rows * queries, tokens), F32),
            pltpu.VMEM((width, rows), BF16),
            pltpu.VMEM((group, depth, tokens), BF16),
            pltpu.SemaphoreType.DMA((4,)),
            pltpu.SemaphoreType.DMA((group // 2,)),
            pltpu.SemaphoreType.DMA((group,)),
        ],
        flops=2 * hidden.size * width_in,
        size=2 * hidden.size,
        out_specs=HBM,
    )(*(pltpu.with_memory_space_constraint(a, pltpu.HBM) for a in inputs))
    got = lax.all_to_all(blocks, ("row", "col"), 0, 0)

    half = width // 2
    n = half * q_dest // group
    feats, precond = call(
        functools.partial(feature_kernel, n_row, n_col, q_dest, width, width_in, n_store),
        (pltpu.HBM((group * n_store, n, tokens), BF16), shape(precond.shape, BF16)),
        [VMEM, HBM],
        [
            pltpu.VMEM((half * q_dest, tokens), F32),
            pltpu.VMEM((group * n_store, n, tokens), BF16),
            pltpu.SemaphoreType.DMA((2,)),
        ],
        size=2 * got.size,
        out_specs=(HBM, VMEM),
    )(got, pltpu.with_memory_space_constraint(precond, pltpu.HBM))
    feats = lax.all_to_all(feats, AXES, 0, 0)

    sources = group * n_store
    part = shape((n_row // 2, n_col, sources, j_width), F32)
    keep, send = call(
        functools.partial(condition_kernel, n_row, n_col, n_store, q_dest),
        (part, part),
        [VMEM, VMEM],
        [pltpu.VMEM((sources * n, tokens), F32)],
        size=2 * precond.size,
    )(feats, precond)
    got = swap(send, "row", n_row, 1)
    diag = [(r * n_col + c, (r ^ 2) * n_col + (c ^ 1)) for r in range(n_row) for c in range(n_col)]
    piece = shape((sources, j_width), F32)
    mine, to_x, to_y, to_xy = call(fold_kernel, (piece,) * 4, [VMEM] * 2, size=keep.size * 8)(keep, got)
    terms = (mine, swap(to_x, "row", n_row, 2), swap(to_y, "col", n_col, 1), lax.ppermute(to_xy, ("row", "col"), diag))
    cond = call(finish_kernel, shape(piece.shape, BF16), [VMEM] * 4, size=mine.size * 8)(*terms)

    cond = jnp.stack([cond] + [swap(cond, "store", n_store, k) for k in range(1, n_store)])
    from_x = swap(cond, "row", n_row, 2)
    from_y = swap(cond, "col", n_col, 1)
    from_xy = lax.ppermute(cond, ("row", "col"), diag)
    scores = shape((sources * q_dest, stored.shape[0]), F32)
    score = functools.partial(score_kernel, n_row, n_col, n_store, q_dest)
    near = jnp.stack([cond, from_x])
    far = swap(near, "row", n_row, 1)
    part = call(functools.partial(score, 0, False), scores, [VMEM] * 3, size=stored.size)(near, far, stored)
    near = jnp.stack([from_y, from_xy])
    far = swap(near, "row", n_row, 1)
    held = pltpu.VMEM((stored.shape[0] // 128, sources * q_dest, 128), F32)
    return call(functools.partial(score, 1, True), scores, [VMEM] * 4, [held], size=stored.size)(near, far, stored, part)


def plain_device(hidden, out_grads, proj_out, proj_in, lengths, precond, stored):
    queries, token_part, columns = hidden.shape
    width_in = proj_in.shape[1]
    local_proj = jnp.einsum("qtc,cb->qtb", hidden, proj_in, preferred_element_type=F32).astype(BF16)
    flattened = local_proj.reshape(queries, token_part * width_in)
    inputs_all = lax.all_gather(flattened, "row", axis=1, tiled=True).reshape(queries, -1, width_in)
    tokens = inputs_all.shape[1]
    position = jnp.arange(tokens, dtype=jnp.int32)
    live_mask = (position[None, :] < lengths[:, None]).astype(F32)
    outputs_proj = jnp.einsum("rqt,ra->qta", out_grads, proj_out, preferred_element_type=F32)
    outputs_proj = (outputs_proj * live_mask[:, :, None]).astype(BF16)
    partial_value = jnp.einsum("qta,qtb->qab", outputs_proj, inputs_all, preferred_element_type=F32)
    partial_value = partial_value.reshape(queries, -1) * tokens ** (-0.5)
    shares = lax.psum_scatter(partial_value, ("row", "col"), scatter_dimension=1, tiled=True).astype(BF16)
    cond_terms = jnp.dot(shares, lax.all_gather(precond, "store", axis=1, tiled=True), preferred_element_type=F32)
    conditioned = lax.psum_scatter(cond_terms, ("row", "col"), scatter_dimension=1, tiled=True).astype(BF16)
    full_features = lax.all_gather(conditioned, ("row", "col"), axis=1, tiled=True)
    return lax.dot_general(
        lax.all_gather(full_features, "store", axis=0, tiled=True),
        stored,
        NT,
        preferred_element_type=F32,
    )


def solution(mesh):
    sizes = tuple(mesh.shape[a] for a in AXES)
    group = sizes[0] * sizes[1]

    def on_device(hidden, out_grads, proj_out, proj_in, lengths, precond, stored):
        args = (hidden, out_grads, proj_out, proj_in, lengths, precond, stored)
        queries = hidden.shape[0]
        fits = sizes[0] == 4 and sizes[1] == 2 and sizes[2] & (sizes[2] - 1) == 0
        fits = fits and queries % group == 0 and queries // group == sizes[0]
        fits = fits and proj_in.shape[1] * sizes[1] == 128 and proj_out.shape[1] * 2 == 128
        fits = fits and stored.shape[0] % 128 == 0 and out_grads.shape[2] == 128 and queries // group * hidden.shape[1] == 128
        if fits:
            return split_device(sizes, *args)
        return plain_device(*args)

    return jax.shard_map(
        on_device,
        mesh=mesh,
        in_specs=(
            P("store", "row", "col"),
            P("row", "store", None),
            P("row", None),
            P("col", None),
            P("store"),
            P(("row", "col"), "store"),
            P(("row", "col", "store"), None),
        ),
        out_specs=P(None, ("row", "col", "store")),
        check_vma=False,
    )
```

```python
import functools

import jax
import jax.numpy as jnp
from jax import lax
from jax.experimental import pallas as pl
from jax.experimental.pallas import tpu as pltpu
from jax.sharding import PartitionSpec as P

F32 = jnp.float32
BF16 = jnp.bfloat16
AXES = ("row", "col", "store")
CHIPS = 4
NT = (((1,), (1,)), ((), ()))
NN = (((1,), (0,)), ((), ()))
VMEM = pl.BlockSpec(memory_space=pltpu.VMEM)
HBM = pl.BlockSpec(memory_space=pltpu.HBM)


def dot(a, b, dims):
    return lax.dot_general(a, b, dims, preferred_element_type=F32)


def offset(k, row, col):
    return lax.bitwise_xor(row, 2 * (k % 2)), lax.bitwise_xor(col, k // 2)


def project_kernel(n_row, n_col, lengths, hidden, proj_in_t, grads, proj_out, *refs):
    outs, scratch = refs[:CHIPS], refs[CHIPS:]
    lengths_s, hidden_s, proj_s, grads_s, weights_s, grads_f32, weights, sems, chunk_sems = scratch
    rows, queries, tokens = grads.shape
    columns = hidden.shape[2]
    t_part = hidden.shape[1]
    width = proj_out.shape[1]
    width_in = proj_in_t.shape[0]
    q_dest = queries // (n_row * n_col)
    share = q_dest // n_col
    row, col = lax.axis_index("row"), lax.axis_index("col")
    pairs = ((proj_in_t, proj_s), (proj_out, weights_s), (grads, grads_s), (lengths, lengths_s))
    small = [pltpu.make_async_copy(src, dst, sems.at[i]) for i, (src, dst) in enumerate(pairs)]
    chunks, starts = [], []
    for k in range(CHIPS):
        r, c = offset(k, row, col)
        for core in range(2):
            first = ((r // 2 * 2 + core) * n_col + c) * q_dest
            i = 2 * k + core
            starts.append(first)
            part = hidden_s.at[pl.ds(i * q_dest, q_dest)]
            chunks.append(pltpu.make_async_copy(hidden.at[pl.ds(first, q_dest)], part, chunk_sems.at[i]))
    for copy in small + chunks:
        copy.start()
    small[0].wait()
    proj = proj_s[...].astype(F32).T.astype(BF16)
    for copy in small[1:]:
        copy.wait()
    i = lax.broadcasted_iota(jnp.int32, (width, width), 0)
    j = lax.broadcasted_iota(jnp.int32, (width, width), 1)
    half = width // 2
    pick = j == jnp.where(i < half, 2 * i, 2 * (i - half) + 1)
    weights[...] = dot(pick.astype(BF16), weights_s[...], NT).astype(BF16)
    grads_f32[...] = grads_s[...].astype(F32).reshape(rows * queries, tokens)
    lane = lax.broadcasted_iota(jnp.int32, (width, tokens), 1)
    for k in range(CHIPS):
        for core in range(2):
            for i in range(share):
                q = starts[2 * k + core] + col * share + i
                g = grads_f32[pl.ds(q, rows, stride=queries), :].astype(BF16)
                u = jnp.where(lane < lengths_s[q], dot(weights[...], g, NN), 0.0)
                at = width_in + i * width
                outs[k][core, at : at + width, :] = u.astype(BF16)
        chunks[2 * k].wait()
        chunks[2 * k + 1].wait()
        part = hidden_s[2 * k * q_dest : 2 * (k + 1) * q_dest]
        v = dot(part.reshape(2 * q_dest * t_part, columns), proj, NN)
        for core in range(2):
            outs[k][core, 0:width_in, :] = v[core * tokens : (core + 1) * tokens].T.astype(BF16)


def feature_kernel(n_row, n_col, q_dest, width, width_in, copies, *refs):
    got, (precond, out, near, held, made, sem) = refs[: 2 * CHIPS], refs[2 * CHIPS :]
    fetch = pltpu.make_async_copy(precond, near, sem.at[1])
    fetch.start()
    tokens = got[0].shape[2]
    t_part = tokens // q_dest
    share = q_dest // n_col
    half = width // 2
    scale = tokens ** (-0.5)
    row, col = lax.axis_index("row"), lax.axis_index("col")
    core = lax.rem(row, 2)
    sides = [[] for _ in range(n_col)]
    for k in range(CHIPS):
        r, _ = offset(k, row, col)
        for side in range(2):
            sides[k // 2].append((lax.bitwise_xor(r, side), got[side * CHIPS + k]))
    parts = [[(b, ref[core, 0:width_in, :].astype(F32)) for b, ref in sides[c]] for c in range(n_col)]
    segment = lax.broadcasted_iota(jnp.int32, (width_in, tokens), 1) // t_part
    lane_f = lax.broadcasted_iota(jnp.int32, (half, n_col * width_in), 1)
    for dy in range(n_col):
        for i in range(share):
            q = lax.bitwise_xor(col, dy) * share + i
            v_rows = []
            for c in range(n_col):
                v = jnp.zeros((width_in, tokens), F32)
                for b, part in parts[c]:
                    shift = lax.rem(b - q + n_row, n_row) * t_part
                    v = jnp.where(segment == b, pltpu.roll(part, shift, 1), v)
                v_rows.append(v)
            v_all = jnp.concatenate(v_rows, axis=0).astype(BF16)
            at = width_in + i * width
            total = None
            for _, ref in sides[dy]:
                term = dot(ref[core, at : at + width, :], v_all, NT)
                total = term if total is None else total + term
            total = total + pltpu.roll(total, width_in, 1)
            packed = jnp.where(lane_f < width_in, total[:half], total[half:]) * scale
            held[pl.ds(q, half, stride=q_dest), :] = packed
    group = n_row * n_col
    n = held.shape[0] // group
    for r in range(group):
        block = held[r * n : (r + 1) * n, :].astype(BF16)
        for k in range(copies):
            made[r * copies + k] = block
    copy = pltpu.make_async_copy(made, out, sem.at[0])
    copy.start()
    copy.wait()
    fetch.wait()


def condition_kernel(n_row, n_col, n_store, q_dest, got, precond, keep, send, got_f32):
    sources, rows, lanes = got.shape
    got_f32[...] = got[...].astype(F32).reshape(sources * rows, lanes)
    core = lax.rem(lax.axis_index("row"), 2)
    group = n_row * n_col
    width = keep.shape[3]
    for ref, side in ((send, 1 - core), (keep, core)):
        columns = []
        for i in range(rows // q_dest):
            blocks = []
            for h in range(n_row // 2):
                for s in range(n_store):
                    at = s * rows + i * q_dest + 2 * h + side
                    blocks.append(got_f32[pl.ds(at, group, stride=n_store * rows), :])
            columns.append(jnp.concatenate(blocks, axis=0).astype(BF16))
        acc = dot(jnp.concatenate(columns, axis=1), precond[...], NN)
        for h in range(n_row // 2):
            for y in range(n_col):
                ref[h, y] = acc[h * sources : (h + 1) * sources, y * width : (y + 1) * width]


def fold_kernel(keep, got, *refs):
    x, y = lax.axis_index("row") // 2, lax.axis_index("col")
    for ref, (a, b) in zip(refs, ((x, y), (1 - x, y), (x, 1 - y), (1 - x, 1 - y))):
        ref[...] = keep[a, b] + got[a, b]


def finish_kernel(*refs):
    total = refs[0][...]
    for ref in refs[1:-1]:
        total += ref[...]
    refs[-1][...] = total.astype(BF16)


def score_kernel(n_row, n_col, n_store, q_dest, iy, last, near, far, stored, *refs):
    n_x, _, sources, width = near.shape
    row, col, store = (lax.axis_index(a) for a in AXES)
    x, core = row // 2, lax.rem(row, 2)
    acc = None
    for iz in range(n_store):
        y, z = lax.bitwise_xor(col, iy), lax.bitwise_xor(store, iz)
        at = pl.multiple_of((z * n_col + y) * width, width)
        left = jnp.concatenate([ref[ix, iz] for ref in (near, far) for ix in range(n_x)], axis=0)
        term = dot(left, stored[:, pl.ds(at, width)], NT)
        acc = term if acc is None else acc + term
    if not last:
        refs[0][...] = acc
        return
    before, out, ordered = refs
    acc += before[...]
    lanes = ordered.shape[2]
    for i in range(ordered.shape[0]):
        for side in range(2):
            for ix in range(n_x):
                q4 = lax.bitwise_xor(x, ix) * 2 + lax.bitwise_xor(core, side)
                base = (side * n_x + ix) * sources
                block = acc[base : base + sources, i * lanes : (i + 1) * lanes]
                ordered[i, pl.ds(q4, sources, stride=q_dest), :] = block
        out[:, i * lanes : (i + 1) * lanes] = ordered[i]


def call(kernel, outs, in_specs, scratch=(), flops=0, size=0, vmem=12, **more):
    return pl.pallas_call(
        kernel,
        out_shape=outs,
        in_specs=in_specs,
        scratch_shapes=list(scratch),
        cost_estimate=pl.CostEstimate(flops=flops, bytes_accessed=size, transcendentals=0),
        compiler_params=pltpu.CompilerParams(vmem_limit_bytes=vmem << 20),
        **more,
    )


def shape(s, t):
    return jax.ShapeDtypeStruct(s, t)


def swap(x, axis, n, k):
    return lax.ppermute(x, axis, [(i, i ^ k) for i in range(n)])


def to_chips(arrays, n_row, n_col):
    diag = [(r * n_col + c, (r ^ 2) * n_col + (c ^ 1)) for r in range(n_row) for c in range(n_col)]
    own, x, y, xy = arrays
    return own, swap(x, "row", n_row, 2), swap(y, "col", n_col, 1), lax.ppermute(xy, ("row", "col"), diag)


def split_device(sizes, hidden, out_grads, proj_out, proj_in, lengths, precond, stored):
    n_row, n_col, n_store = sizes
    group = n_row * n_col
    queries, t_part, columns = hidden.shape
    rows, _, tokens = out_grads.shape
    width, width_in = proj_out.shape[1], proj_in.shape[1]
    q_dest = queries // group
    share = q_dest // n_col
    depth = width_in + share * width
    col = lax.axis_index("col")
    j_width = precond.shape[1] // n_col

    inputs = (lengths, hidden, proj_in.T, out_grads, proj_out)
    blocks = call(
        functools.partial(project_kernel, n_row, n_col),
        (shape((2, depth, tokens), BF16),) * CHIPS,
        [HBM] * 5,
        [
            pltpu.SMEM(lengths.shape, jnp.int32),
            pltpu.VMEM(hidden.shape, BF16),
            pltpu.VMEM((width_in, columns), BF16),
            pltpu.VMEM(out_grads.shape, BF16),
            pltpu.VMEM(proj_out.shape, BF16),
            pltpu.VMEM((rows * queries, tokens), F32),
            pltpu.VMEM((width, rows), BF16),
            pltpu.SemaphoreType.DMA((4,)),
            pltpu.SemaphoreType.DMA((2 * CHIPS,)),
        ],
        flops=2 * hidden.size * width_in,
        size=2 * hidden.size,
        out_specs=(VMEM,) * CHIPS,
    )(*(pltpu.with_memory_space_constraint(a, pltpu.HBM) for a in inputs))
    near = to_chips(blocks, n_row, n_col)
    far = [swap(a, "row", n_row, 1) for a in near]

    half = width // 2
    n = half * q_dest // group
    feats, precond = call(
        functools.partial(feature_kernel, n_row, n_col, q_dest, width, width_in, n_store),
        (pltpu.HBM((group * n_store, n, tokens), BF16), shape(precond.shape, BF16)),
        [VMEM] * (2 * CHIPS) + [HBM],
        [
            pltpu.VMEM((half * q_dest, tokens), F32),
            pltpu.VMEM((group * n_store, n, tokens), BF16),
            pltpu.SemaphoreType.DMA((2,)),
        ],
        size=2 * precond.size,
        out_specs=(HBM, VMEM),
    )(*near, *far, pltpu.with_memory_space_constraint(precond, pltpu.HBM))
    feats = lax.all_to_all(feats, AXES, 0, 0)

    sources = group * n_store
    part = shape((n_row // 2, n_col, sources, j_width), F32)
    keep, send = call(
        functools.partial(condition_kernel, n_row, n_col, n_store, q_dest),
        (part, part),
        [VMEM, VMEM],
        [pltpu.VMEM((sources * n, tokens), F32)],
        size=2 * precond.size,
    )(feats, precond)
    got = swap(send, "row", n_row, 1)
    piece = shape((sources, j_width), F32)
    terms = call(fold_kernel, (piece,) * 4, [VMEM] * 2, size=keep.size * 8)(keep, got)
    terms = to_chips(terms, n_row, n_col)
    cond = call(finish_kernel, shape(piece.shape, BF16), [VMEM] * 4, size=keep.size * 8)(*terms)

    cond = jnp.stack([cond] + [swap(cond, "store", n_store, k) for k in range(1, n_store)])
    cond, from_x, from_y, from_xy = to_chips([cond] * CHIPS, n_row, n_col)
    scores = shape((sources * q_dest, stored.shape[0]), F32)
    score = functools.partial(score_kernel, n_row, n_col, n_store, q_dest)
    near = jnp.stack([cond, from_x])
    far = swap(near, "row", n_row, 1)
    part = call(functools.partial(score, 0, False), scores, [VMEM] * 3, size=stored.size)(near, far, stored)
    near = jnp.stack([from_y, from_xy])
    far = swap(near, "row", n_row, 1)
    held = pltpu.VMEM((stored.shape[0] // 128, sources * q_dest, 128), F32)
    return call(functools.partial(score, 1, True), scores, [VMEM] * 4, [held], size=stored.size)(near, far, stored, part)


def plain_device(hidden, out_grads, proj_out, proj_in, lengths, precond, stored):
    queries, token_part, columns = hidden.shape
    width_in = proj_in.shape[1]
    local_proj = jnp.einsum("qtc,cb->qtb", hidden, proj_in, preferred_element_type=F32).astype(BF16)
    flattened = local_proj.reshape(queries, token_part * width_in)
    inputs_all = lax.all_gather(flattened, "row", axis=1, tiled=True).reshape(queries, -1, width_in)
    tokens = inputs_all.shape[1]
    position = jnp.arange(tokens, dtype=jnp.int32)
    live_mask = (position[None, :] < lengths[:, None]).astype(F32)
    outputs_proj = jnp.einsum("rqt,ra->qta", out_grads, proj_out, preferred_element_type=F32)
    outputs_proj = (outputs_proj * live_mask[:, :, None]).astype(BF16)
    partial_value = jnp.einsum("qta,qtb->qab", outputs_proj, inputs_all, preferred_element_type=F32)
    partial_value = partial_value.reshape(queries, -1) * tokens ** (-0.5)
    shares = lax.psum_scatter(partial_value, ("row", "col"), scatter_dimension=1, tiled=True).astype(BF16)
    cond_terms = jnp.dot(shares, lax.all_gather(precond, "store", axis=1, tiled=True), preferred_element_type=F32)
    conditioned = lax.psum_scatter(cond_terms, ("row", "col"), scatter_dimension=1, tiled=True).astype(BF16)
    full_features = lax.all_gather(conditioned, ("row", "col"), axis=1, tiled=True)
    return lax.dot_general(
        lax.all_gather(full_features, "store", axis=0, tiled=True),
        stored,
        NT,
        preferred_element_type=F32,
    )


def solution(mesh):
    sizes = tuple(mesh.shape[a] for a in AXES)
    group = sizes[0] * sizes[1]

    def on_device(hidden, out_grads, proj_out, proj_in, lengths, precond, stored):
        args = (hidden, out_grads, proj_out, proj_in, lengths, precond, stored)
        queries = hidden.shape[0]
        fits = sizes[0] == 4 and sizes[1] == 2 and sizes[2] & (sizes[2] - 1) == 0
        fits = fits and queries % group == 0 and queries // group == sizes[0]
        fits = fits and proj_in.shape[1] * sizes[1] == 128 and proj_out.shape[1] * 2 == 128
        fits = fits and stored.shape[0] % 128 == 0 and out_grads.shape[2] == 128 and queries // group * hidden.shape[1] == 128
        if fits:
            return split_device(sizes, *args)
        return plain_device(*args)

    return jax.shard_map(
        on_device,
        mesh=mesh,
        in_specs=(
            P("store", "row", "col"),
            P("row", "store", None),
            P("row", None),
            P("col", None),
            P("store"),
            P(("row", "col"), "store"),
            P(("row", "col", "store"), None),
        ),
        out_specs=P(None, ("row", "col", "store")),
        check_vma=False,
    )
```
